128 devices in a mesh: comp: 2 (over core), tile: 64 (over z, y, x).
Axes of the slice: x: 4, y: 4, z: 4, core: 2. Of those that a mesh axis runs over, the one named last changes fastest.
Arguments:
- state: float32 [2, 72, 524288], P('comp', None, 'tile'), may hold values from -6 to 6
- diffusivity: float32 [2, 72, 524288], P('comp', None, 'tile'), may hold values from 0.1 to 0.48
- surface: bfloat16 [2, 16, 524288], P('comp', None, 'tile'), may hold values from -6 to 6
- remap_weights: bfloat16 [2, 4096, 4, 128, 128], P('comp', 'tile'), may hold values from -0.25 to 0.25
- send_table: int32 [2, 64, 64, 8], P(None, 'tile'), may hold values from 0 to 63
- recv_slot: int32 [2, 4096, 4], P('comp', 'tile'), may hold values from 0 to 511, as said below
- profile: bfloat16 [2, 72, 16], P('comp'), may hold values from -1.5 to 1.5
Outputs:
- new_state: float32 [2, 72, 524288], P('comp', None, 'tile')
- remapped: bfloat16 [2, 16, 524288], P('comp', None, 'tile')
The draws below stay inside these ranges and needn't reach their ends.
Inputs may be any that keep to these rules, and one draw needn't show every extreme that they name: p = recv_slot[c, B, k] names slot p % 8 of source device p // 8; the 256 values of one destination device are distinct, and in every draw some source device fills all 8 slots of some destination device.
All inputs are finite; a program needn't handle non-finite values.
Results may differ from the reference program's by a relative error of at most 0.0025.
The reference program's roundings to bfloat16 on the way count: a program that leaves them out, or rounds other values in their place, can miss the bound.
Values may be sent and summed in bfloat16 or wider, within the bound.
No kernel may reach another device: no remote copies, remote signals or barrier semaphores. Data moves between devices by JAX's collectives and lax.ppermute only.
A program may use at most 128 MiB of HBM per device.

```python
import math
import jax
import jax.numpy as jnp
from jax import lax

LEV = 72
NF = 16
TB = 128
KB = 4
SUB = 10
NBLK_DEV = 64
CAP = 8
NBLK = 4096
NCELL = 524288
N_TILE = 64


def device_routing(key):
    key_perm, key_forced, key_shuffle, key_block, key_fill = jax.random.split(key, 5)
    total = N_TILE * CAP
    requests = NBLK_DEV * KB
    position = jnp.arange(total, dtype=jnp.int32)
    ranking = jax.random.permutation(key_perm, total).astype(jnp.int32)
    forced = jax.random.randint(key_forced, (), 0, N_TILE, dtype=jnp.int32)
    scores = jnp.where(position // CAP == forced, position % CAP, CAP + ranking)
    chosen = jnp.argsort(scores, stable=True)[:requests].astype(jnp.int32)
    shuffle = jax.random.permutation(key_shuffle, requests)
    placed = chosen[shuffle]
    source = jax.random.randint(key_block, (requests,), 0, NBLK_DEV, dtype=jnp.int32)
    filler = jax.random.randint(key_fill, (total,), 0, NBLK_DEV, dtype=jnp.int32)
    inverse = filler.at[placed].set(source)
    return (placed, inverse)


def routing_tables(key):
    base = jax.random.fold_in(key, 7001)
    recv_list = []
    send_list = []
    for component in range(2):
        keys = jax.random.split(jax.random.fold_in(base, component), N_TILE)
        placed, inverse = jax.vmap(device_routing)(keys)
        recv_list.append(placed.reshape(N_TILE * NBLK_DEV, KB))
        send_list.append(jnp.transpose(inverse.reshape(N_TILE, N_TILE, CAP), (1, 0, 2)))
    return (jnp.stack(recv_list), jnp.stack([send_list[1], send_list[0]]))


def draw_send_table(key, part):
    return routing_tables(key)[1].astype(jnp.int32)


def draw_recv_slot(key, part):
    return routing_tables(key)[0].astype(jnp.int32)


def shard_levels(rng, shape, shards, low, largest):
    level = 1.0
    for dim, parts in shards:
        draws = jax.random.uniform(jax.random.fold_in(jax.random.fold_in(rng, 6), dim), (parts,), jnp.float32, low / len(shards), largest / len(shards))
        level = level * jnp.repeat(jnp.exp(draws), shape[dim] // parts).reshape((-1,) + (1,) * (len(shape) - 1 - dim))
    return level


def normal_values(own_key, dims, deviation, limit, pieces=(), kind=jnp.bfloat16):
    drawn = jax.random.normal(own_key, dims, jnp.float32) * deviation
    if len(pieces) > 0:
        drawn = shard_levels(own_key, dims, pieces, -0.22, 0.18) * drawn
    return jnp.clip(drawn, min=-limit, max=limit).astype(kind)


def setup_inputs(seed: int = 0) -> dict:
    arg_keys = jax.random.split(jax.random.key(seed), 8)
    return {
        "state": normal_values(arg_keys[0], (2, LEV, NCELL), 1.0, 6.0, ((0, 2), (2, 64)), jnp.float32),
        "diffusivity": jnp.clip(jnp.exp(math.log(0.48) - 1.5686159 * jax.random.uniform(arg_keys[1], (2, LEV, NCELL), jnp.float32) ** shard_levels(arg_keys[1], (2, LEV, NCELL), ((0, 2), (2, 64)), -0.2, 0.2)), 0.1, 0.48),
        "surface": normal_values(arg_keys[2], (2, NF, NCELL), 1.0, 6.0, ((0, 2), (2, 64))),
        "remap_weights": normal_values(arg_keys[3], (2, NBLK, KB, TB, TB), (KB * TB) ** -0.5, 0.25, ((0, 2), (1, 64))),
        "send_table": draw_send_table(jax.random.fold_in(arg_keys[7], 71), 0),
        "recv_slot": draw_recv_slot(jax.random.fold_in(arg_keys[7], 71), 0),
        "profile": normal_values(arg_keys[6], (2, LEV, NF), NF ** -0.5, 1.5, ((0, 2),)),
    }


def reference(state, diffusivity, surface, remap_weights, send_table, recv_slot, profile):
    states_out = []
    remaps_out = []
    for component in range(2):
        opposite = 1 - component
        positions = recv_slot[component]
        src_dev = positions // CAP
        slot_index = positions % CAP
        target_dev = (jnp.arange(NBLK, dtype=jnp.int32) // NBLK_DEV)[:, None]
        local_block = send_table[opposite][src_dev, target_dev, slot_index]
        source_block = (src_dev * NBLK_DEV + local_block).astype(jnp.int32)
        blocks = surface[opposite].reshape(NF, NBLK, TB)
        weights = remap_weights[component]

        def one_group(group):
            start = (group * NBLK_DEV).astype(jnp.int32)
            group_blocks = lax.dynamic_slice_in_dim(source_block, start, NBLK_DEV, 0)
            group_weights = lax.dynamic_slice_in_dim(weights, start, NBLK_DEV, 0)
            sources = jnp.take(blocks, group_blocks, axis=1)
            return jnp.einsum("fbki,bkij->fbj", sources.astype(jnp.float32), group_weights.astype(jnp.float32))

        grouped = lax.map(one_group, jnp.arange(N_TILE, dtype=jnp.int32))
        remapped = jnp.transpose(grouped, (1, 0, 2, 3)).reshape(NF, NCELL).astype(jnp.bfloat16)
        evolved = state[component]
        coefficients = diffusivity[component]
        for substep in range(SUB):
            left_cell = jnp.roll(evolved, 1, axis=1)
            right_cell = jnp.roll(evolved, -1, axis=1)
            evolved = evolved + coefficients * (left_cell - 2.0 * evolved + right_cell)
        tendency = jnp.dot(profile[component], remapped, preferred_element_type=jnp.float32)
        states_out.append(evolved + tendency)
        remaps_out.append(remapped)
    return jnp.stack(states_out), jnp.stack(remaps_out)
```

```python
import jax
import jax.numpy as jnp
from jax import lax
from jax.experimental import pallas as pl
from jax.experimental.pallas import tpu as pltpu
from jax.sharding import PartitionSpec as P

DEPTH = 10
LANES = 128
SUBL = 8


def pack_kernel(table_ref, src_ref, out_ref):
    sender = 1 - lax.axis_index("comp")
    base = pl.program_id(0) * out_ref.shape[0]
    capacity = table_ref.shape[1]
    fields = src_ref.shape[0]

    def one(d, carry):
        for s in range(capacity):
            b = table_ref[sender, s, base + d]
            start = pl.multiple_of(b * LANES, LANES)
            out_ref[d, s * fields : (s + 1) * fields, :] = src_ref[:, pl.ds(start, LANES)]
        return carry

    lax.fori_loop(0, out_ref.shape[0], one, 0)


def pack(table, src, tiles):
    fields, cells = src.shape
    capacity = table.shape[1]
    step = 16
    return pl.pallas_call(
        pack_kernel,
        out_shape=jax.ShapeDtypeStruct((tiles, capacity * fields, LANES), src.dtype),
        grid_spec=pltpu.PrefetchScalarGridSpec(
            num_scalar_prefetch=1,
            grid=(tiles // step,),
            in_specs=[pl.BlockSpec((fields, cells), lambda i, t: (0, 0))],
            out_specs=pl.BlockSpec((step, capacity * fields, LANES), lambda i, t: (i, 0, 0)),
        ),
        cost_estimate=pl.CostEstimate(flops=0, transcendentals=0, bytes_accessed=3 << 20),
        name="pack",
    )(table, src)


def stencil_kernel(x_ref, k_ref, left_ref, right_ref, out_ref, xs, ks):
    cells = x_ref.shape[1]
    xs[:, :LANES] = left_ref[0]
    ks[:, :LANES] = left_ref[1]
    xs[:, LANES : LANES + cells] = x_ref[...]
    ks[:, LANES : LANES + cells] = k_ref[...]
    xs[:, LANES + cells :] = right_ref[0]
    ks[:, LANES + cells :] = right_ref[1]
    chunk = 1024
    wide = chunk + 2 * LANES

    def one(c, carry):
        start = pl.multiple_of(c * chunk, chunk)
        x = xs[:, pl.ds(start, wide)]
        k = ks[:, pl.ds(start, wide)]
        for _ in range(DEPTH):
            left = pltpu.roll(x, 1, 1)
            right = pltpu.roll(x, wide - 1, 1)
            x = x + k * (left - 2.0 * x + right)
        out_ref[:, pl.ds(start, chunk)] = x[:, LANES : LANES + chunk]
        return carry

    lax.fori_loop(0, cells // chunk, one, 0)


def stencil(x, k, left, right):
    levels, cells = x.shape
    row = pl.BlockSpec((SUBL, cells), lambda i: (i, 0))
    rim = pl.BlockSpec((2, SUBL, LANES), lambda i: (0, i, 0))
    return pl.pallas_call(
        stencil_kernel,
        out_shape=jax.ShapeDtypeStruct(x.shape, x.dtype),
        grid=(levels // SUBL,),
        in_specs=[row, row, rim, rim],
        out_specs=row,
        scratch_shapes=[pltpu.VMEM((SUBL, cells + 2 * LANES), jnp.float32)] * 2,
        cost_estimate=pl.CostEstimate(
            flops=60 * levels * cells, transcendentals=0, bytes_accessed=12 * levels * cells
        ),
        name="stencil",
    )(x, k, left, right)


def remap_kernel(slot_ref, recv_ref, w_ref, profile_ref, evolved_ref, new_ref, remapped_ref):
    blocks = w_ref.shape[0]
    sources = w_ref.shape[1]
    base = pl.program_id(0) * blocks
    profile = profile_ref[...]
    for b in range(blocks):
        parts = [recv_ref[slot_ref[k, base + b]] for k in range(sources)]
        picked = jnp.concatenate(parts, axis=1)
        weights = w_ref[b].reshape(sources * LANES, LANES)
        mixed = jnp.dot(picked, weights, preferred_element_type=jnp.float32)
        rounded = mixed.astype(jnp.bfloat16)
        cols = slice(b * LANES, (b + 1) * LANES)
        remapped_ref[:, cols] = rounded
        new_ref[:, cols] = evolved_ref[:, cols] + jnp.dot(
            profile, rounded, preferred_element_type=jnp.float32
        )


def remap(slots, recv, weights, profile, evolved):
    levels, cells = evolved.shape
    blocks, sources = weights.shape[:2]
    fields = recv.shape[1]
    step = 8
    width = step * LANES
    return pl.pallas_call(
        remap_kernel,
        out_shape=(
            jax.ShapeDtypeStruct((levels, cells), jnp.float32),
            jax.ShapeDtypeStruct((fields, cells), jnp.bfloat16),
        ),
        grid_spec=pltpu.PrefetchScalarGridSpec(
            num_scalar_prefetch=1,
            grid=(blocks // step,),
            in_specs=[
                pl.BlockSpec(recv.shape, lambda i, s: (0, 0, 0)),
                pl.BlockSpec((step,) + weights.shape[1:], lambda i, s: (i, 0, 0, 0)),
                pl.BlockSpec(profile.shape, lambda i, s: (0, 0)),
                pl.BlockSpec((levels, width), lambda i, s: (0, i)),
            ],
            out_specs=[
                pl.BlockSpec((levels, width), lambda i, s: (0, i)),
                pl.BlockSpec((fields, width), lambda i, s: (0, i)),
            ],
        ),
        cost_estimate=pl.CostEstimate(
            flops=2 * weights.size * fields, transcendentals=0, bytes_accessed=16 << 20
        ),
        name="remap",
    )(slots, recv, weights, profile, evolved)


def on_device(state, diffusivity, surface, remap_weights, send_table, recv_slot, profile):
    tiles = lax.axis_size("tile")
    x, k = state[0], diffusivity[0]
    fields = surface.shape[1]
    capacity = send_table.shape[3]
    swapped = lax.ppermute(surface[0], "comp", [(0, 1), (1, 0)])
    table = jnp.transpose(send_table[:, 0], (0, 2, 1))
    packed = pack(table, swapped, tiles)
    received = lax.all_to_all(packed, "tile", 0, 0, tiled=True)

    up = [(i, (i + 1) % tiles) for i in range(tiles)]
    down = [(j, i) for i, j in up]
    last = jnp.stack([x[:, -LANES:], k[:, -LANES:]])
    first = jnp.stack([x[:, :LANES], k[:, :LANES]])
    left = lax.ppermute(last, "tile", up)
    right = lax.ppermute(first, "tile", down)
    evolved = stencil(x, k, left, right)

    slots = jnp.transpose(recv_slot[0], (1, 0))
    recv = received.reshape(tiles * capacity, fields, LANES)
    updated, remapped = remap(slots, recv, remap_weights[0], profile[0], evolved)
    return (updated[None], remapped[None])


def solution(mesh):
    in_specs = (
        P("comp", None, "tile"),
        P("comp", None, "tile"),
        P("comp", None, "tile"),
        P("comp", "tile", None, None, None),
        P(None, "tile", None, None),
        P("comp", "tile", None),
        P("comp", None, None),
    )
    out_specs = (P("comp", None, "tile"), P("comp", None, "tile"))
    return jax.shard_map(
        on_device, mesh=mesh, in_specs=in_specs, out_specs=out_specs, check_vma=False
    )
```
